256 devices in a mesh: ctx: 32 (over z, x), head: 8 (over y, core).
Axes of the slice: x: 4, y: 4, z: 8, core: 2. Of those that a mesh axis runs over, the one named last changes fastest.
Arguments:
- queries: bfloat16 [16384, 4096], P('ctx', 'head'), may hold values from -6 to 6
- key_states: bfloat16 [16384, 512], P('ctx', 'head'), may hold values from -6 to 6
- value_states: bfloat16 [16384, 512], P('ctx', 'head'), may hold values from -6 to 6
- attn_out: bfloat16 [16384, 4096], P('ctx', 'head'), may hold values from -2 to 2
- grad_out: bfloat16 [16384, 4096], P('ctx', 'head'), may hold values from -6 to 6
- log_norm: float32 [32, 16384], P('head', 'ctx'), as said below
- doc_lengths: int32 [64], replicated, may hold values from 1 to 2048, as said below
Outputs:
- grad_queries: bfloat16 [16384, 4096], P('ctx', 'head')
- grad_keys: bfloat16 [16384, 512], P('ctx', 'head')
- grad_values: bfloat16 [16384, 512], P('ctx', 'head')
The draws below stay inside these ranges and needn't reach their ends.
Inputs may be any that keep to these rules, and one draw needn't show every extreme that they name: `doc_lengths`: 64 document lengths that add up to 16384; one document has exactly 2048 tokens. `log_norm`: a given input, not recomputed from the others.
All inputs are finite; a program needn't handle non-finite values.
Results may differ from the reference program's by a relative error of at most 0.0051.
Values may be sent and summed in bfloat16 or wider, within the bound.
A program may use at most 64 MiB of HBM per device.

```python
import jax
import jax.numpy as jnp
from jax import lax

DH = 128
GROUP = 8
QH = 32
KVH = 4
TOK_DEV = 512
TOKENS = 16384
MOST = 2048
NDOCS = 64


def doc_cuts(key):
    folded = jax.random.fold_in(key, 11)
    key_offset, key_rank, key_guard = jax.random.split(folded, 3)
    groups = TOKENS // MOST
    offset = jax.random.randint(key_offset, (), 1, MOST).astype(jnp.int32)
    chosen = jax.random.randint(key_guard, (), 0, groups - 1).astype(jnp.int32)
    guarded = offset + MOST * chosen
    places = jnp.arange(TOKENS, dtype=jnp.int32)
    lattice = offset + MOST * jnp.arange(groups, dtype=jnp.int32)
    inside = (places > guarded) & (places < guarded + MOST)
    allowed = (places >= 1) & ((places - offset) % MOST != 0) & jnp.logical_not(inside)
    random_rank = jax.random.randint(key_rank, (TOKENS,), 0, 16384).astype(jnp.int32)
    scores = jnp.where(allowed, random_rank * TOKENS + places, -1 - places)
    picked = lax.top_k(scores, NDOCS - groups - 1)[1].astype(jnp.int32)
    cut_points = jnp.sort(jnp.concatenate([lattice, picked]))
    bounds = jnp.concatenate([jnp.zeros((1,), jnp.int32), cut_points, jnp.full((1,), TOKENS, jnp.int32)])
    return (bounds[1:] - bounds[:-1]).astype(jnp.int32)


def draw_doc_lengths(key, part):
    return doc_cuts(key)


def draw_log_norm(key, part):
    lengths = doc_cuts(key)
    doc_ends = jnp.cumsum(lengths).astype(jnp.int32)
    places = jnp.arange(TOKENS, dtype=jnp.int32)
    starts = jnp.sum(jnp.where(doc_ends[None, :] <= places[:, None], lengths[None, :], 0), axis=1)
    counts = (places - starts + 1).astype(jnp.float32)
    noise_key = jax.random.fold_in(key, 23)
    spread = jax.random.uniform(noise_key, (QH, TOKENS), jnp.float32)
    level = 0.5 + spread
    return (jnp.log(counts)[None, :] + level).astype(jnp.float32)


def levels(rng, shape, cuts, least, top_value):
    def one(axis_at, blocks):
        draws = jax.random.uniform(jax.random.fold_in(jax.random.fold_in(rng, 6), axis_at), (blocks,), jnp.float32, least / len(cuts), top_value / len(cuts))
        return jnp.repeat(jnp.exp(draws), shape[axis_at] // blocks).reshape((-1,) + (1,) * (len(shape) - axis_at - 1))

    factor_of = one(*cuts[0])
    for cut in cuts[1:]:
        factor_of = factor_of * one(*cut)
    return factor_of


def normal_values(stream_key, extent, scale, limit, cuts=(), kind=jnp.bfloat16):
    drawn = jax.random.normal(stream_key, extent, jnp.float32) * scale
    if len(cuts) > 0:
        drawn = levels(stream_key, extent, cuts, -0.22, 0.18) * drawn
    return jnp.clip(drawn, min=-limit, max=limit).astype(kind)


def setup_inputs(seed: int = 0) -> dict:
    splits = jax.random.split(jax.random.key(seed), 8)
    queries = normal_values(splits[0], (TOKENS, QH * DH), 1.0, 6.0, ((0, 32), (1, 8)))
    key_states = normal_values(splits[1], (TOKENS, KVH * DH), 1.0, 6.0, ((0, 32), (1, 8)))
    value_states = normal_values(splits[2], (TOKENS, KVH * DH), 1.0, 6.0, ((0, 32), (1, 8)))
    attn_out = normal_values(splits[3], (TOKENS, QH * DH), 0.3, 2.0, ((0, 32), (1, 8)))
    grad_out = normal_values(splits[4], (TOKENS, QH * DH), 1.0, 6.0, ((0, 32), (1, 8)))
    log_norm = draw_log_norm(jax.random.fold_in(splits[7], 71), 0)
    doc_lengths = draw_doc_lengths(jax.random.fold_in(splits[7], 71), 0)
    return dict(queries=queries, key_states=key_states, value_states=value_states, attn_out=attn_out, grad_out=grad_out, log_norm=log_norm, doc_lengths=doc_lengths)


def reference(queries, key_states, value_states, attn_out, grad_out, log_norm, doc_lengths):
    score_scale = DH ** -0.5
    tile_rows = min(512, TOK_DEV)
    block_count = TOKENS // tile_rows
    window_len = MOST + tile_rows
    places = jnp.arange(TOKENS, dtype=jnp.int32)
    doc_ends = jnp.cumsum(doc_lengths).astype(jnp.int32)
    starts = jnp.sum(jnp.where(doc_ends[None, :] <= places[:, None], doc_lengths[None, :], 0), axis=1).astype(jnp.int32)
    query_heads = queries.astype(jnp.float32).reshape(TOKENS, KVH, GROUP, DH)
    grad_heads = grad_out.astype(jnp.float32).reshape(TOKENS, KVH, GROUP, DH)
    row_delta = jnp.sum((attn_out.astype(jnp.float32) * grad_out.astype(jnp.float32)).reshape(TOKENS, QH, DH), axis=-1)
    row_delta = row_delta.reshape(TOKENS, KVH, GROUP)
    norm_heads = jnp.transpose(log_norm).reshape(TOKENS, KVH, GROUP)
    front = jnp.zeros((MOST, KVH, DH), jnp.float32)
    key_padded = jnp.concatenate([front, key_states.astype(jnp.float32).reshape(TOKENS, KVH, DH)], axis=0)
    value_padded = jnp.concatenate([front, value_states.astype(jnp.float32).reshape(TOKENS, KVH, DH)], axis=0)
    high = lax.Precision.HIGHEST

    def one_block(carried, block_index):
        key_grads, value_grads = carried
        first_row = (block_index * tile_rows).astype(jnp.int32)
        tile_queries = lax.dynamic_slice_in_dim(query_heads, first_row, tile_rows, 0)
        tile_grads = lax.dynamic_slice_in_dim(grad_heads, first_row, tile_rows, 0)
        tile_norm = jnp.transpose(lax.dynamic_slice_in_dim(norm_heads, first_row, tile_rows, 0), (1, 2, 0))
        tile_delta = jnp.transpose(lax.dynamic_slice_in_dim(row_delta, first_row, tile_rows, 0), (1, 2, 0))
        query_pos = first_row + jnp.arange(tile_rows, dtype=jnp.int32)
        query_start = lax.dynamic_slice_in_dim(starts, first_row, tile_rows, 0)
        tile_keys = lax.dynamic_slice_in_dim(key_padded, first_row, window_len, 0)
        tile_values = lax.dynamic_slice_in_dim(value_padded, first_row, window_len, 0)
        key_pos = first_row - MOST + jnp.arange(window_len, dtype=jnp.int32)
        allowed = (key_pos[None, :] <= query_pos[:, None]) & (key_pos[None, :] >= query_start[:, None])
        scores = jnp.einsum('qagd,kad->agqk', tile_queries, tile_keys, precision=high) * score_scale
        probs = jnp.where(allowed[None, None], jnp.exp(scores - tile_norm[..., None]), jnp.float32(0.0))
        dprobs = jnp.einsum('qagd,kad->agqk', tile_grads, tile_values, precision=high)
        dscores = probs * (dprobs - tile_delta[..., None])
        probs_b = lax.optimization_barrier(probs.astype(jnp.bfloat16)).astype(jnp.float32)
        dscores_b = lax.optimization_barrier(dscores.astype(jnp.bfloat16)).astype(jnp.float32)
        value_part = jnp.einsum('agqk,qagd->kad', probs_b, tile_grads, precision=high)
        key_part = jnp.einsum('agqk,qagd->kad', dscores_b, tile_queries, precision=high)
        query_part = jnp.einsum('agqk,kad->qagd', dscores_b, tile_keys, precision=high)
        previous = lax.dynamic_slice_in_dim(key_grads, first_row, window_len, 0)
        key_grads = lax.dynamic_update_slice_in_dim(key_grads, previous + key_part, first_row, 0)
        previous = lax.dynamic_slice_in_dim(value_grads, first_row, window_len, 0)
        value_grads = lax.dynamic_update_slice_in_dim(value_grads, previous + value_part, first_row, 0)
        return (key_grads, value_grads), query_part

    empty = jnp.zeros((MOST + TOKENS, KVH, DH), jnp.float32)
    (key_grads, value_grads), query_parts = lax.scan(one_block, (empty, empty), jnp.arange(block_count, dtype=jnp.int32))
    grad_queries = (query_parts.reshape(TOKENS, QH * DH) * score_scale).astype(jnp.bfloat16)
    grad_keys = (key_grads[MOST:].reshape(TOKENS, KVH * DH) * score_scale).astype(jnp.bfloat16)
    grad_values = value_grads[MOST:].reshape(TOKENS, KVH * DH).astype(jnp.bfloat16)
    return (grad_queries, grad_keys, grad_values)
```

```python
import functools

import jax
import jax.numpy as jnp
from jax import lax
from jax.experimental import pallas as pl
from jax.experimental.pallas import tpu as pltpu
from jax.sharding import PartitionSpec as P

MESH = pl.DeviceIdType.MESH
LOG2E = 1.4426950408889634
NT = (((1,), (1,)), ((), ()))
NN = (((1,), (0,)), ((), ()))
SPAN = 4
ORDER = (0, 1, 3, 2, 4)


def mm(a, b, dims):
    return lax.dot_general(a, b, dims, preferred_element_type=jnp.float32)


def kernel(
    doc_ref, q_hbm, k_hbm, v_hbm, o_hbm, do_hbm, ln_hbm,
    dq_hbm, dk_hbm, dv_hbm,
    q, o, do, ln, qt, dot, dl, st, hb, kn, vn, kt, g, pr, sb, rb, dqt, dq, dk, dv,
    in_sem, out_sem, hs_sem, hr_sem, ps_sem, pr_sem, gs_sem, gr_sem, is_sem, ir_sem,
):
    rows, heads = q.shape[0], qt.shape[0]
    dim = q.shape[1] // heads
    half = dim // 2
    mid = rows // 2
    n_ctx = lax.axis_size("ctx")
    scale = dim ** (-0.5)
    me = lax.axis_index("ctx")
    head = lax.axis_index("head")
    core = lax.rem(head, 2)
    pair = head + 1 - 2 * core

    def at(shift):
        return lax.rem(me + shift + n_ctx, n_ctx)

    loads = [
        pltpu.make_async_copy(src, dst, in_sem.at[n])
        for n, (src, dst) in enumerate(
            (
                (k_hbm, hb.at[0, core, 0:half]), (v_hbm, hb.at[0, core, half:dim]),
                (q_hbm, q), (do_hbm, do), (o_hbm, o), (ln_hbm, ln),
            )
        )
    ]
    for c in loads:
        c.start()

    barrier = pltpu.get_barrier_semaphore()
    pl.semaphore_signal(barrier, inc=1, device_id=(me, pair), device_id_type=MESH)
    for d in range(1, SPAN + 1):
        pl.semaphore_signal(barrier, inc=1, device_id=(at(d), head), device_id_type=MESH)
        pl.semaphore_signal(barrier, inc=1, device_id=(at(-d), head), device_id_type=MESH)

    pos = me * rows + lax.broadcasted_iota(jnp.int32, (1, rows), 1)

    def one_doc(j, carry):
        end, start = carry
        end = end + doc_ref[j]
        return end, jnp.where(pos >= end, end, start)

    _, start = lax.fori_loop(
        0, doc_ref.shape[0], one_doc, (jnp.int32(0), jnp.zeros((1, rows), jnp.int32))
    )
    st[...] = start

    for c in loads:
        c.wait()
    for h in range(heads):
        cols = slice(h * dim, (h + 1) * dim)
        qt[h] = q[:, cols].T
        dot[h] = do[:, cols].T
        dl[h : h + 1, :] = jnp.sum(
            dot[h].astype(jnp.float32) * o[:, cols].T.astype(jnp.float32), axis=0, keepdims=True
        )
    ln[...] = ln[...] * LOG2E

    pl.semaphore_wait(barrier, 1 + 2 * SPAN)

    def to_pair(src, dst, send, recv):
        return pltpu.make_async_remote_copy(
            src, dst, send, recv, device_id=(me, pair), device_id_type=MESH
        )

    def fwd(d):
        return to_pair(hb.at[d, core], hb.at[d, core], ps_sem.at[d], pr_sem.at[d])

    def ici(d):
        return pltpu.make_async_remote_copy(
            hb.at[0, core], hb.at[d, core], hs_sem.at[d - 1], hr_sem.at[d - 1],
            device_id=(at(d), head), device_id_type=MESH,
        )

    def gpair(d):
        return to_pair(g.at[d, 1 - core], pr.at[d], gs_sem.at[d], gr_sem.at[d])

    def gici(d):
        return pltpu.make_async_remote_copy(
            sb.at[d - 1], rb.at[d - 1], is_sem.at[d - 1], ir_sem.at[d - 1],
            device_id=(at(-d), head), device_id_type=MESH,
        )

    fwd(0).start()
    for d in ORDER[1:]:
        ici(d).start()

    def one_head(d, h, first):
        cols = slice(h * dim, (h + 1) * dim)
        if d == 0:
            parts = ((0, mid, 0, rows), (mid, rows, mid, rows))
        elif d == SPAN:
            parts = ((0, mid, 0, mid), (mid, rows, 0, rows))
        else:
            parts = ((0, rows, 0, rows),)
        seen = set()
        for klo, khi, qlo, qhi in parts:
            size = (khi - klo, qhi - qlo)
            s = mm(kn[klo:khi, :], q[qlo:qhi, cols], NT)
            dp = mm(vn[klo:khi, :], do[qlo:qhi, cols], NT)
            kpos = (me - d) * rows + klo + lax.broadcasted_iota(jnp.int32, size, 0)
            allowed = kpos >= st[:, qlo:qhi]
            if d == 0:
                qpos = me * rows + qlo + lax.broadcasted_iota(jnp.int32, size, 1)
                allowed = allowed & (kpos <= qpos)
            p = jnp.where(
                allowed, jnp.exp2(s * (scale * LOG2E) - ln[h : h + 1, qlo:qhi]), 0.0
            )
            ds = p * (dp - dl[h : h + 1, qlo:qhi])
            pb = p.astype(jnp.bfloat16)
            dsb = ds.astype(jnp.bfloat16)
            gk = mm(qt[h, :, qlo:qhi], dsb, NT)
            gv = mm(dot[h, :, qlo:qhi], pb, NT)
            for c in range(2):
                part = jnp.concatenate(
                    [gk[c * half : (c + 1) * half], gv[c * half : (c + 1) * half]], axis=0
                )
                if h == 0:
                    g[d, c, :, klo:khi] = part
                else:
                    g[d, c, :, klo:khi] += part
            gq = mm(kt[:, klo:khi], dsb, NN)
            if first and not seen:
                dqt[h, :, qlo:qhi] = gq
            else:
                dqt[h, :, qlo:qhi] += gq
            seen.add(klo)

    for i, d in enumerate(ORDER):
        fwd(d).wait_recv()
        kt[...] = jnp.concatenate([hb[d, 0, :half], hb[d, 1, :half]], axis=0)
        kn[...] = kt[...].T
        vn[...] = jnp.concatenate([hb[d, 0, half:], hb[d, 1, half:]], axis=0).T
        for h in range(heads):
            if h == heads // 2:
                if i + 1 < len(ORDER):
                    nxt = ORDER[i + 1]
                    ici(nxt).wait_recv()
                    fwd(nxt).start()
                if i >= 1 and ORDER[i - 1] != 0:
                    prev = ORDER[i - 1]
                    gpair(prev).wait_recv()
                    sb[prev - 1] = (g[prev, core] + pr[prev]).astype(jnp.bfloat16)
            if h == heads // 2 + 1 and i >= 1 and ORDER[i - 1] != 0:
                gici(ORDER[i - 1]).start()
            one_head(d, h, i == 0)
        gpair(d).start()

    stores = [
        pltpu.make_async_copy(src, dst, out_sem.at[n])
        for n, (src, dst) in enumerate(((dq, dq_hbm), (dk, dk_hbm), (dv, dv_hbm)))
    ]
    last = ORDER[-1]
    for h in range(heads // 2):
        dq[:, h * dim : (h + 1) * dim] = (dqt[h].T * scale).astype(jnp.bfloat16)
    gpair(last).wait_recv()
    sb[last - 1] = (g[last, core] + pr[last]).astype(jnp.bfloat16)
    for h in range(heads // 2, heads):
        dq[:, h * dim : (h + 1) * dim] = (dqt[h].T * scale).astype(jnp.bfloat16)
    gici(last).start()
    stores[0].start()
    gpair(0).wait_recv()
    total = g[0, core] + pr[0]
    for d in ORDER[1:]:
        gici(d).wait_recv()
        total = total + rb[d - 1].astype(jnp.float32)
    dk[...] = (total[:half] * scale).astype(jnp.bfloat16)
    dv[...] = total[half:].astype(jnp.bfloat16)
    stores[1].start()
    stores[2].start()
    for d in range(SPAN + 1):
        fwd(d).wait_send()
        gpair(d).wait_send()
        if d:
            ici(d).wait_send()
            gici(d).wait_send()
    for c in stores:
        c.wait()


def local(queries, key_states, value_states, attn_out, grad_out, log_norm, doc_lengths):
    rows, half = key_states.shape
    dim = 2 * half
    heads = queries.shape[1] // dim
    bf, f32 = jnp.bfloat16, jnp.float32
    blocks = SPAN + 1
    anywhere = pl.BlockSpec(memory_space=pl.ANY)
    vmem, dma = pltpu.VMEM, pltpu.SemaphoreType.DMA
    grad_q, grad_k, grad_v = pl.pallas_call(
        kernel,
        out_shape=(
            jax.ShapeDtypeStruct((rows, heads * dim), bf),
            jax.ShapeDtypeStruct((half, rows), bf),
            jax.ShapeDtypeStruct((half, rows), bf),
        ),
        in_specs=[pl.BlockSpec(memory_space=pltpu.SMEM)] + [anywhere] * 6,
        out_specs=(anywhere,) * 3,
        scratch_shapes=[
            vmem((rows, heads * dim), bf),
            vmem((rows, heads * dim), bf),
            vmem((rows, heads * dim), bf),
            vmem((heads, rows), f32),
            vmem((heads, dim, rows), bf),
            vmem((heads, dim, rows), bf),
            vmem((heads, rows), f32),
            vmem((1, rows), jnp.int32),
            vmem((blocks, 2, dim, rows), bf),
            vmem((rows, dim), bf),
            vmem((rows, dim), bf),
            vmem((dim, rows), bf),
            vmem((blocks, 2, dim, rows), f32),
            vmem((blocks, dim, rows), f32),
            vmem((SPAN, dim, rows), bf),
            vmem((SPAN, dim, rows), bf),
            vmem((heads, dim, rows), f32),
            vmem((rows, heads * dim), bf),
            vmem((half, rows), bf),
            vmem((half, rows), bf),
            dma((6,)), dma((3,)),
            dma((SPAN,)), dma((SPAN,)), dma((blocks,)), dma((blocks,)),
            dma((blocks,)), dma((blocks,)), dma((SPAN,)), dma((SPAN,)),
        ],
        compiler_params=pltpu.CompilerParams(
            collective_id=0, has_side_effects=True, vmem_limit_bytes=60 * 2**20
        ),
    )(doc_lengths, queries, key_states.T, value_states.T, attn_out, grad_out, log_norm)
    return grad_q, grad_k.T, grad_v.T


def solution(mesh):
    in_specs = (
        P("ctx", "head"), P("ctx", "head"), P("ctx", "head"), P("ctx", "head"),
        P("ctx", "head"), P("head", "ctx"), P(),
    )
    out_specs = (P("ctx", "head"), P("ctx", "head"), P("ctx", "head"))
    return jax.shard_map(local, mesh=mesh, in_specs=in_specs, out_specs=out_specs, check_vma=False)
```

```python
import jax
import jax.numpy as jnp
from jax import lax
from jax.experimental import pallas as pl
from jax.experimental.pallas import tpu as pltpu
from jax.sharding import PartitionSpec as P

MESH = pl.DeviceIdType.MESH
LOG2E = 1.4426950408889634
NT = (((1,), (1,)), ((), ()))
NN = (((1,), (0,)), ((), ()))
SPAN = 4
GATHER = (4, 1, 2, 3)
BLOCKS = (1, 2, 3)
RETURN = (1, 2, 3, 4)


def mm(a, b, dims):
    return lax.dot_general(a, b, dims, preferred_element_type=jnp.float32)


def kernel(
    doc_ref, q_hbm, k_hbm, v_hbm, o_hbm, do_hbm, ln_hbm,
    dq_hbm, dk_hbm, dv_hbm,
    kv, q, do, o, qt, dot, ln, dl, st, hb, kn, vn, kt, g, r0, sb, rb, dqt, dqi, dq, dk, dv,
    in_sem, out_sem, ps_sem, pr_sem, hs_sem, hr_sem, gs_sem, gr_sem, qs_sem, qr_sem,
):
    part = q.shape[2]
    rows = 2 * part
    heads = qt.shape[1]
    dim = qt.shape[3]
    half = dim // 2
    n_ctx = lax.axis_size("ctx")
    scale = dim ** (-0.5)
    me = lax.axis_index("ctx")
    head = lax.axis_index("head")
    core = lax.rem(head, 2)
    base = head - core
    pair = base + 1 - core

    pieces = []
    for i in range(2):
        at = pl.ds(i * part, part)
        pieces += [
            (k_hbm.at[:, at], kv.at[i, 0:half]),
            (v_hbm.at[:, at], kv.at[i, half:dim]),
            (q_hbm.at[at], q.at[0, i]),
            (do_hbm.at[at], do.at[0, i]),
            (o_hbm.at[at], o.at[i]),
            (ln_hbm.at[:, at], ln.at[0, i]),
        ]
    loads = [pltpu.make_async_copy(s, d, in_sem.at[n]) for n, (s, d) in enumerate(pieces)]
    for c in loads:
        c.start()

    barrier = pltpu.get_barrier_semaphore()
    pl.semaphore_signal(barrier, inc=1, device_id=(me, pair), device_id_type=MESH)
    expected = jnp.int32(1)
    for d in range(1, SPAN + 1):

        @pl.when(me >= d)
        def _():
            for c in range(2):
                pl.semaphore_signal(
                    barrier, inc=1, device_id=(me - d, base + c), device_id_type=MESH
                )

        @pl.when(me + d < n_ctx)
        def _():
            for c in range(2):
                pl.semaphore_signal(
                    barrier, inc=1, device_id=(me + d, base + c), device_id_type=MESH
                )

        expected = expected + jnp.where(me >= d, 2, 0) + jnp.where(me + d < n_ctx, 2, 0)

    dqt[...] = jnp.zeros_like(dqt)
    g[0] = jnp.zeros(g.shape[1:], g.dtype)
    g[SPAN] = jnp.zeros(g.shape[1:], g.dtype)

    places = [
        me * rows + i * part + lax.broadcasted_iota(jnp.int32, (1, part), 1) for i in range(2)
    ]

    def one_doc(j, carry):
        end, a, b = carry
        end = end + doc_ref[j]
        return end, jnp.where(places[0] >= end, end, a), jnp.where(places[1] >= end, end, b)

    none = jnp.zeros((1, part), jnp.int32)
    _, st[0], st[1] = lax.fori_loop(0, doc_ref.shape[0], one_doc, (jnp.int32(0), none, none))

    for c in loads:
        c.wait()
    hb[0, core] = kv[core]

    def turn(slot):
        for i in range(2):
            for h in range(heads):
                cols = slice(h * dim, (h + 1) * dim)
                qt[slot, h, i] = q[slot, i, :, cols].T
                dot[slot, h, i] = do[slot, i, :, cols].T

    turn(0)
    for i in range(2):
        for h in range(heads):
            cols = slice(h * dim, (h + 1) * dim)
            dl[0, i, h : h + 1, :] = jnp.sum(
                dot[0, h, i].astype(jnp.float32) * o[i, :, cols].T.astype(jnp.float32),
                axis=0,
                keepdims=True,
            )

    pl.semaphore_wait(barrier, expected)

    def remote(src, dst, send, recv, ctx, dev):
        return pltpu.make_async_remote_copy(
            src, dst, send, recv, device_id=(ctx, dev), device_id_type=MESH
        )

    swaps = [
        remote(s, d, ps_sem.at[n], pr_sem.at[n], me, pair)
        for n, (s, d) in enumerate(
            (
                (kv.at[1 - core], hb.at[0, core]),
                (q.at[0], q.at[1]),
                (do.at[0], do.at[1]),
                (ln.at[0], ln.at[1]),
                (dl.at[0], dl.at[1]),
                (g.at[0, 1 - core], r0),
            )
        )
    ]

    def ahead(d, c):
        return remote(
            kv.at[c], hb.at[d, core], hs_sem.at[d - 1, c], hr_sem.at[d - 1, core],
            me + d, base + c,
        )

    def arrived(d, s):
        return remote(
            kv.at[0], hb.at[d, s], hs_sem.at[d - 1, 0], hr_sem.at[d - 1, s], me, pair
        )

    def back(d, c):
        return remote(
            sb.at[d - 1, c], rb.at[d - 1, core], gs_sem.at[d - 1, c], gr_sem.at[d - 1, core],
            me - d, base + c,
        )

    def returned(d, s):
        return remote(
            sb.at[d - 1, 0], rb.at[d - 1, s], gs_sem.at[d - 1, 0], gr_sem.at[d - 1, s], me, pair
        )

    def hand(h):
        return remote(dqt.at[1, h], dqi.at[h], qs_sem.at[h], qr_sem.at[h], me, pair)

    swaps[0].start()
    for d in GATHER:

        @pl.when(me + d < n_ctx)
        def _():
            for c in range(2):
                ahead(d, c).start()

    for c in swaps[1:5]:
        c.start()

    def await_block(d):
        @pl.when(me >= d)
        def _():
            for s in range(2):
                arrived(d, s).wait_recv()

        @pl.when(me < d)
        def _():
            hb[d] = jnp.zeros(hb.shape[1:], hb.dtype)

    def take(d):
        kt[...] = jnp.concatenate([hb[d, 0, :half], hb[d, 1, :half]], axis=0)
        kn[...] = kt[...].T
        vn[...] = jnp.concatenate([hb[d, 0, half:], hb[d, 1, half:]], axis=0).T

    krow = lax.broadcasted_iota(jnp.int32, (part, part), 0)
    qcol = lax.broadcasted_iota(jnp.int32, (part, part), 1)

    def one_head(d, slot, h, halves, causal, fresh):
        cols = slice(h * dim, (h + 1) * dim)
        first = (me - d) * rows + core * part
        total = None
        for i in halves:
            s = mm(kn[...], q[slot, i, :, cols], NT)
            dp = mm(vn[...], do[slot, i, :, cols], NT)
            allowed = krow >= st[i] - first
            if causal:
                allowed = allowed & (krow <= qcol)
            p = jnp.where(
                allowed,
                jnp.exp2(s * (scale * LOG2E) - ln[slot, i, h : h + 1, :] * LOG2E),
                0.0,
            )
            ds = p * (dp - dl[slot, i, h : h + 1, :])
            pb = p.astype(jnp.bfloat16)
            dsb = ds.astype(jnp.bfloat16)
            gk = mm(qt[slot, h, i], dsb, NT)
            gv = mm(dot[slot, h, i], pb, NT)
            total = (gk, gv) if total is None else (total[0] + gk, total[1] + gv)
            dqt[slot, h, i] += mm(kt[...], dsb, NN)
        gk, gv = total
        for c in range(2):
            dims = slice(c * half, (c + 1) * half)
            if fresh:
                g[d, c, 0:half] = gk[dims]
                g[d, c, half:dim] = gv[dims]
            else:
                g[d, c, 0:half] += gk[dims]
                g[d, c, half:dim] += gv[dims]

    def give(d):
        @pl.when(me >= d)
        def _():
            for c in range(2):
                back(d, c).start()

    swaps[0].wait_recv()
    take(0)
    for h in range(heads):
        one_head(0, 0, h, (core,), True, False)
    for c in swaps[1:5]:
        c.wait_recv()
    turn(1)
    for h in range(heads):
        one_head(0, 1, h, (core,), True, False)

    await_block(SPAN)
    side = SPAN * core
    take(side)
    for slot in range(2):
        for h in range(heads):
            one_head(side, slot, h, (1 - core,), False, False)
    swaps[5].start()

    pending = None
    for d in BLOCKS:
        await_block(d)
        take(d)
        if pending is not None:
            give(pending)
        for slot in range(2):
            for h in range(heads):
                one_head(d, slot, h, (0, 1), False, slot == 0 and h == 0)
        sb[d - 1] = g[d].astype(jnp.bfloat16)
        pending = d

    take(SPAN)
    give(pending)
    for h in range(heads):
        one_head(SPAN, 1, h, (core,), False, False)
        if h:
            hand(h - 1).start()
    for h in range(heads):
        one_head(SPAN, 0, h, (core,), False, False)
        if h == 0:
            hand(heads - 1).start()
    sb[SPAN - 1] = g[SPAN].astype(jnp.bfloat16)

    stores = []
    for i in range(2):
        at = pl.ds(i * part, part)
        stores += [(dq.at[i], dq_hbm.at[at]), (dk.at[i], dk_hbm.at[:, at]), (dv.at[i], dv_hbm.at[:, at])]
    stores = [pltpu.make_async_copy(s, d, out_sem.at[n]) for n, (s, d) in enumerate(stores)]

    for h in range(heads):
        hand(h).wait_recv()
        if h == 0:
            give(SPAN)
        for i in range(2):
            dq[i, :, h * dim : (h + 1) * dim] = (
                (dqt[0, h, i] + dqi[h, i]).T * scale
            ).astype(jnp.bfloat16)
    stores[0].start()
    stores[3].start()

    swaps[5].wait_recv()
    sums = [g[0, core], r0[...]]
    for d in RETURN:

        @pl.when(me + d < n_ctx)
        def _():
            for s in range(2):
                returned(d, s).wait_recv()

        @pl.when(me + d >= n_ctx)
        def _():
            rb[d - 1] = jnp.zeros(rb.shape[1:], rb.dtype)

        sums[0] = sums[0] + rb[d - 1, core].astype(jnp.float32)
        sums[1] = sums[1] + rb[d - 1, 1 - core].astype(jnp.float32)
    for i, total in ((core, sums[0]), (1 - core, sums[1])):
        dk[i] = (total[:half] * scale).astype(jnp.bfloat16)
        dv[i] = total[half:].astype(jnp.bfloat16)
    for n in (1, 2, 4, 5):
        stores[n].start()

    for c in swaps:
        c.wait_send()
    for h in range(heads):
        hand(h).wait_send()
    for d in range(1, SPAN + 1):

        @pl.when(me + d < n_ctx)
        def _():
            for c in range(2):
                ahead(d, c).wait_send()

        @pl.when(me >= d)
        def _():
            for c in range(2):
                back(d, c).wait_send()

    for c in stores:
        c.wait()


def local(queries, key_states, value_states, attn_out, grad_out, log_norm, doc_lengths):
    rows, half = key_states.shape
    dim = 2 * half
    part = rows // 2
    heads = queries.shape[1] // dim
    wide = heads * dim
    bf, f32 = jnp.bfloat16, jnp.float32
    blocks = SPAN + 1
    anywhere = pl.BlockSpec(memory_space=pl.ANY)
    vmem, dma = pltpu.VMEM, pltpu.SemaphoreType.DMA
    grad_q, grad_k, grad_v = pl.pallas_call(
        kernel,
        out_shape=(
            jax.ShapeDtypeStruct((rows, wide), bf),
            jax.ShapeDtypeStruct((half, rows), bf),
            jax.ShapeDtypeStruct((half, rows), bf),
        ),
        in_specs=[pl.BlockSpec(memory_space=pltpu.SMEM)] + [anywhere] * 6,
        out_specs=(anywhere,) * 3,
        scratch_shapes=[
            vmem((2, dim, part), bf),
            vmem((2, 2, part, wide), bf),
            vmem((2, 2, part, wide), bf),
            vmem((2, part, wide), bf),
            vmem((2, heads, 2, dim, part), bf),
            vmem((2, heads, 2, dim, part), bf),
            vmem((2, 2, heads, part), f32),
            vmem((2, 2, heads, part), f32),
            vmem((2, 1, part), jnp.int32),
            vmem((blocks, 2, dim, part), bf),
            vmem((part, dim), bf),
            vmem((part, dim), bf),
            vmem((dim, part), bf),
            vmem((blocks, 2, dim, part), f32),
            vmem((dim, part), f32),
            vmem((SPAN, 2, dim, part), bf),
            vmem((SPAN, 2, dim, part), bf),
            vmem((2, heads, 2, dim, part), f32),
            vmem((heads, 2, dim, part), f32),
            vmem((2, part, wide), bf),
            vmem((2, half, part), bf),
            vmem((2, half, part), bf),
            dma((12,)), dma((6,)), dma((6,)), dma((6,)),
            dma((SPAN, 2)), dma((SPAN, 2)), dma((SPAN, 2)), dma((SPAN, 2)),
            dma((heads,)), dma((heads,)),
        ],
        compiler_params=pltpu.CompilerParams(
            collective_id=0, has_side_effects=True, vmem_limit_bytes=60 * 2**20
        ),
    )(doc_lengths, queries, key_states.T, value_states.T, attn_out, grad_out, log_norm)
    return grad_q, grad_k.T, grad_v.T


def solution(mesh):
    in_specs = (
        P("ctx", "head"), P("ctx", "head"), P("ctx", "head"), P("ctx", "head"),
        P("ctx", "head"), P("head", "ctx"), P(),
    )
    out_specs = (P("ctx", "head"), P("ctx", "head"), P("ctx", "head"))
    return jax.shard_map(local, mesh=mesh, in_specs=in_specs, out_specs=out_specs, check_vma=False)
```

```python
import jax
import jax.numpy as jnp
from jax import lax
from jax.experimental import pallas as pl
from jax.experimental.pallas import tpu as pltpu
from jax.sharding import PartitionSpec as P

MESH = pl.DeviceIdType.MESH
LOG2E = 1.4426950408889634
NT = (((1,), (1,)), ((), ()))
NN = (((1,), (0,)), ((), ()))
SPAN = 4
GATHER = (4, 1, 3, 2)
BLOCKS = (1, 2, 3)
RETURN = (1, 2, 3, 4)
RELAY = (2, 3)


def mm(a, b, dims):
    return lax.dot_general(a, b, dims, preferred_element_type=jnp.float32)


def kernel(
    doc_ref, q_hbm, k_hbm, v_hbm, o_hbm, do_hbm, ln_hbm,
    dq_hbm, dk_hbm, dv_hbm,
    kv, q, do, o, ln, dl, st, hb, kn, vn, kt, pb, dsb, g, g0, r0, sb, rb, dqt, dqi, dq, dk, dv,
    in_sem, out_sem, ps_sem, pr_sem, hs_sem, hr_sem, gs_sem, gr_sem, qs_sem, qr_sem, re_sem,
):
    part = q.shape[2]
    rows = 2 * part
    heads = dqt.shape[1]
    dim = dqt.shape[3]
    half = dim // 2
    n_ctx = lax.axis_size("ctx")
    scale = dim ** (-0.5)
    me = lax.axis_index("ctx")
    head = lax.axis_index("head")
    core = lax.rem(head, 2)
    ring = lax.rem(me, SPAN)
    base = head - core
    pair = base + 1 - core

    pieces = []
    for i in range(2):
        at = pl.ds(i * part, part)
        pieces += [
            (k_hbm.at[:, at], kv.at[i, 0:half]),
            (v_hbm.at[:, at], kv.at[i, half:dim]),
            (q_hbm.at[at], q.at[0, i]),
            (do_hbm.at[at], do.at[0, i]),
            (o_hbm.at[at], o.at[i]),
            (ln_hbm.at[:, at], ln.at[0, i]),
        ]
    loads = [pltpu.make_async_copy(s, d, in_sem.at[n]) for n, (s, d) in enumerate(pieces)]
    for c in loads:
        c.start()

    barrier = pltpu.get_barrier_semaphore()
    pl.semaphore_signal(barrier, inc=1, device_id=(me, pair), device_id_type=MESH)
    expected = jnp.int32(1)
    for d in range(1, SPAN + 1):

        @pl.when(me >= d)
        def _():
            for c in range(2):
                pl.semaphore_signal(
                    barrier, inc=1, device_id=(me - d, base + c), device_id_type=MESH
                )

        @pl.when(me + d < n_ctx)
        def _():
            for c in range(2):
                pl.semaphore_signal(
                    barrier, inc=1, device_id=(me + d, base + c), device_id_type=MESH
                )

        expected = expected + jnp.where(me >= d, 2, 0) + jnp.where(me + d < n_ctx, 2, 0)

    dqt[...] = jnp.zeros_like(dqt)
    g[0] = jnp.zeros(g.shape[1:], g.dtype)
    g[SPAN] = jnp.zeros(g.shape[1:], g.dtype)

    places = [
        me * rows + i * part + lax.broadcasted_iota(jnp.int32, (1, part), 1) for i in range(2)
    ]

    def one_doc(j, carry):
        end, a, b = carry
        end = end + doc_ref[j]
        return end, jnp.where(places[0] >= end, end, a), jnp.where(places[1] >= end, end, b)

    none = jnp.zeros((1, part), jnp.int32)
    _, st[0], st[1] = lax.fori_loop(0, doc_ref.shape[0], one_doc, (jnp.int32(0), none, none))

    for c in loads:
        c.wait()
    hb[0, core] = kv[core]

    for i in range(2):
        for h in range(heads):
            cols = slice(h * dim, (h + 1) * dim)
            prod = do[0, i, :, cols].astype(jnp.float32) * o[i, :, cols].astype(jnp.float32)
            dl[0, i, h : h + 1, :] = jnp.sum(prod.T, axis=0, keepdims=True)

    pl.semaphore_wait(barrier, expected)

    def remote(src, dst, send, recv, ctx, dev):
        return pltpu.make_async_remote_copy(
            src, dst, send, recv, device_id=(ctx, dev), device_id_type=MESH
        )

    swaps = [
        remote(s, d, ps_sem.at[n], pr_sem.at[n], me, pair)
        for n, (s, d) in enumerate(
            (
                (kv.at[1 - core], hb.at[0, core]),
                (q.at[0], q.at[1]),
                (do.at[0], do.at[1]),
                (ln.at[0], ln.at[1]),
                (dl.at[0], dl.at[1]),
                (g0.at[1 - core], r0),
            )
        )
    ]

    def ahead(d, c):
        return remote(
            kv.at[c], hb.at[d, core], hs_sem.at[d - 1, c], hr_sem.at[d - 1, core],
            me + d, base + c,
        )

    def arrived(d, s):
        return remote(
            kv.at[0], hb.at[d, s], hs_sem.at[d - 1, 0], hr_sem.at[d - 1, s], me, pair
        )

    def sends(d):
        near = me + d < n_ctx
        return near & (ring + d < SPAN) if d in RELAY else near

    def onward(d, s):
        return remote(
            hb.at[SPAN, s], hb.at[d, s], re_sem.at[d - RELAY[0], s], hr_sem.at[d - 1, s],
            me + d - SPAN, head,
        )

    def back(d, c):
        return remote(
            sb.at[d - 1, c], rb.at[d - 1, core], gs_sem.at[d - 1, c], gr_sem.at[d - 1, core],
            me - d, base + c,
        )

    def returned(d, s):
        return remote(
            sb.at[d - 1, 0], rb.at[d - 1, s], gs_sem.at[d - 1, 0], gr_sem.at[d - 1, s], me, pair
        )

    def hand(h):
        return remote(dqt.at[1, h], dqi.at[h], qs_sem.at[h], qr_sem.at[h], me, pair)

    swaps[0].start()
    for d in GATHER:

        @pl.when(sends(d))
        def _():
            for c in range(2):
                ahead(d, c).start()

    for c in swaps[1:5]:
        c.start()

    def await_block(d):
        @pl.when(me >= d)
        def _():
            for s in range(2):
                arrived(d, s).wait_recv()

        @pl.when(me < d)
        def _():
            hb[d] = jnp.zeros(hb.shape[1:], hb.dtype)

    def take(d):
        kt[...] = jnp.concatenate([hb[d, 0, :half], hb[d, 1, :half]], axis=0)
        kn[...] = kt[...].T
        vn[...] = jnp.concatenate([hb[d, 0, half:], hb[d, 1, half:]], axis=0).T

    krow = lax.broadcasted_iota(jnp.int32, (part, part), 0)
    qcol = lax.broadcasted_iota(jnp.int32, (part, part), 1)

    def attend(d, slot, halves, causal, fresh, between=None):
        first = (me - d) * rows + core * part
        for h in range(heads):
            cols = slice(h * dim, (h + 1) * dim)
            for n, i in enumerate(halves):
                s = mm(kn[...], q[slot, i, :, cols], NT)
                dp = mm(vn[...], do[slot, i, :, cols], NT)
                allowed = krow >= st[i] - first
                if causal:
                    allowed = allowed & (krow <= qcol)
                p = jnp.where(
                    allowed,
                    jnp.exp2(s * (scale * LOG2E) - ln[slot, i, h : h + 1, :] * LOG2E),
                    0.0,
                )
                pb[h, n] = p.astype(jnp.bfloat16)
                dsb[h, n] = (p * (dp - dl[slot, i, h : h + 1, :])).astype(jnp.bfloat16)
        if between is not None:
            between()
        gk, gv = (0.0, 0.0) if fresh else (g[d, 0], g[d, 1])
        for h in range(heads):
            cols = slice(h * dim, (h + 1) * dim)
            for n, i in enumerate(halves):
                gk = gk + mm(dsb[h, n], q[slot, i, :, cols], NN)
                gv = gv + mm(pb[h, n], do[slot, i, :, cols], NN)
                dqt[slot, h, i] += mm(kt[...], dsb[h, n], NN)
        g[d, 0], g[d, 1] = gk, gv

    def lay(dst, d):
        gk, gv = g[d, 0].T, g[d, 1].T
        for c in range(2):
            dst[c, 0:half] = gk[c * half : (c + 1) * half].astype(dst.dtype)
            dst[c, half:dim] = gv[c * half : (c + 1) * half].astype(dst.dtype)

    def give(d):
        @pl.when(me >= d)
        def _():
            for c in range(2):
                back(d, c).start()

    swaps[0].wait_recv()
    take(0)
    attend(0, 0, (core,), True, False)
    for c in swaps[1:5]:
        c.wait_recv()
    attend(0, 1, (core,), True, False)

    await_block(SPAN)
    for d in RELAY:

        @pl.when((ring + d >= SPAN) & (me >= SPAN))
        def _():
            for s in range(2):
                onward(d, s).start()

    side = SPAN * core
    take(side)
    for slot in range(2):
        attend(side, slot, (1 - core,), False, False)
    lay(g0, 0)

    pending = None
    for d in BLOCKS:
        await_block(d)
        take(d)
        if pending is None:
            swaps[5].start()
        else:
            give(pending)
        for slot in range(2):
            attend(d, slot, (0, 1), False, slot == 0)
        lay(sb.at[d - 1], d)
        pending = d

    take(SPAN)
    give(pending)
    attend(SPAN, 1, (core,), False, False)

    def hand_over():
        for h in range(heads):
            hand(h).start()

    attend(SPAN, 0, (core,), False, False, hand_over)
    lay(sb.at[SPAN - 1], SPAN)

    stores = []
    for i in range(2):
        at = pl.ds(i * part, part)
        stores += [(dq.at[i], dq_hbm.at[at]), (dk.at[i], dk_hbm.at[:, at]), (dv.at[i], dv_hbm.at[:, at])]
    stores = [pltpu.make_async_copy(s, d, out_sem.at[n]) for n, (s, d) in enumerate(stores)]

    for h in range(heads):
        hand(h).wait_recv()
        if h == 0:
            give(SPAN)
        for i in range(2):
            dq[i, :, h * dim : (h + 1) * dim] = (
                (dqt[0, h, i] + dqi[h, i]).T * scale
            ).astype(jnp.bfloat16)
    stores[0].start()
    stores[3].start()

    swaps[5].wait_recv()
    sums = [g0[core], r0[...]]
    for d in RETURN:

        @pl.when(me + d < n_ctx)
        def _():
            for s in range(2):
                returned(d, s).wait_recv()

        @pl.when(me + d >= n_ctx)
        def _():
            rb[d - 1] = jnp.zeros(rb.shape[1:], rb.dtype)

        sums[0] = sums[0] + rb[d - 1, core].astype(jnp.float32)
        sums[1] = sums[1] + rb[d - 1, 1 - core].astype(jnp.float32)
    for i, total in ((core, sums[0]), (1 - core, sums[1])):
        dk[i] = (total[:half] * scale).astype(jnp.bfloat16)
        dv[i] = total[half:].astype(jnp.bfloat16)
    for n in (1, 2, 4, 5):
        stores[n].start()

    for c in swaps:
        c.wait_send()
    for h in range(heads):
        hand(h).wait_send()
    for d in range(1, SPAN + 1):

        @pl.when(sends(d))
        def _():
            for c in range(2):
                ahead(d, c).wait_send()

        @pl.when(me >= d)
        def _():
            for c in range(2):
                back(d, c).wait_send()

    for d in RELAY:

        @pl.when((ring + d >= SPAN) & (me >= SPAN))
        def _():
            for s in range(2):
                onward(d, s).wait_send()

    for c in stores:
        c.wait()


def finish(dq, dk, dv, dq_out, dk_out, dv_out, sem):
    copies = [
        pltpu.make_async_copy(s, d, sem.at[n])
        for n, (s, d) in enumerate(((dq, dq_out), (dk, dk_out), (dv, dv_out)))
    ]
    for c in copies:
        c.start()
    for c in copies:
        c.wait()


def local(queries, key_states, value_states, attn_out, grad_out, log_norm, doc_lengths):
    rows, half = key_states.shape
    dim = 2 * half
    part = rows // 2
    heads = queries.shape[1] // dim
    wide = heads * dim
    bf, f32 = jnp.bfloat16, jnp.float32
    blocks = SPAN + 1
    anywhere = pl.BlockSpec(memory_space=pl.ANY)
    vmem, dma = pltpu.VMEM, pltpu.SemaphoreType.DMA
    grad_q, grad_k, grad_v = pl.pallas_call(
        kernel,
        out_shape=(
            jax.ShapeDtypeStruct((rows, wide), bf),
            jax.ShapeDtypeStruct((half, rows), bf),
            jax.ShapeDtypeStruct((half, rows), bf),
        ),
        in_specs=[pl.BlockSpec(memory_space=pltpu.SMEM)] + [anywhere] * 6,
        out_specs=(anywhere,) * 3,
        scratch_shapes=[
            vmem((2, dim, part), bf),
            vmem((2, 2, part, wide), bf),
            vmem((2, 2, part, wide), bf),
            vmem((2, part, wide), bf),
            vmem((2, 2, heads, part), f32),
            vmem((2, 2, heads, part), f32),
            vmem((2, 1, part), jnp.int32),
            vmem((blocks, 2, dim, part), bf),
            vmem((part, dim), bf),
            vmem((part, dim), bf),
            vmem((dim, part), bf),
            vmem((heads, 2, part, part), bf),
            vmem((heads, 2, part, part), bf),
            vmem((blocks, 2, part, dim), f32),
            vmem((2, dim, part), f32),
            vmem((dim, part), f32),
            vmem((SPAN, 2, dim, part), bf),
            vmem((SPAN, 2, dim, part), bf),
            vmem((2, heads, 2, dim, part), f32),
            vmem((heads, 2, dim, part), f32),
            vmem((2, part, wide), bf),
            vmem((2, half, part), bf),
            vmem((2, half, part), bf),
            dma((12,)), dma((6,)), dma((6,)), dma((6,)),
            dma((SPAN, 2)), dma((SPAN, 2)), dma((SPAN, 2)), dma((SPAN, 2)),
            dma((heads,)), dma((heads,)), dma((2, 2)),
        ],
        compiler_params=pltpu.CompilerParams(
            collective_id=0, has_side_effects=True, vmem_limit_bytes=40 * 2**20
        ),
    )(doc_lengths, queries, key_states.T, value_states.T, attn_out, grad_out, log_norm)
    grad_q, grad_k, grad_v = pl.pallas_call(
        finish,
        out_shape=(
            jax.ShapeDtypeStruct((rows, wide), bf),
            jax.ShapeDtypeStruct((half, rows), bf),
            jax.ShapeDtypeStruct((half, rows), bf),
        ),
        in_specs=[pl.BlockSpec(memory_space=vmem)] * 3,
        out_specs=(anywhere,) * 3,
        scratch_shapes=[dma((3,))],
        compiler_params=pltpu.CompilerParams(vmem_limit_bytes=2 * 2**20),
    )(grad_q, grad_k, grad_v)
    return grad_q, grad_k.T, grad_v.T


def solution(mesh):
    in_specs = (
        P("ctx", "head"), P("ctx", "head"), P("ctx", "head"), P("ctx", "head"),
        P("ctx", "head"), P("head", "ctx"), P(),
    )
    out_specs = (P("ctx", "head"), P("ctx", "head"), P("ctx", "head"))
    return jax.shard_map(local, mesh=mesh, in_specs=in_specs, out_specs=out_specs, check_vma=False)
```

```python
import jax
import jax.numpy as jnp
from jax import lax
from jax.experimental import pallas as pl
from jax.experimental.pallas import tpu as pltpu
from jax.sharding import PartitionSpec as P

MESH = pl.DeviceIdType.MESH
LOG2E = 1.4426950408889634
NT = (((1,), (1,)), ((), ()))
NN = (((1,), (0,)), ((), ()))
SPAN = 4
GATHER = (4, 1, 3, 2)
BLOCKS = (1, 3, 2)
RETURN = (1, 3, 2, 4)
RELAY = (2, 3)


def mm(a, b, dims):
    return lax.dot_general(a, b, dims, preferred_element_type=jnp.float32)


def kernel(
    doc_ref, q_hbm, k_hbm, v_hbm, o_hbm, do_hbm, ln_hbm,
    dq_hbm, dk_hbm, dv_hbm,
    kv, q, do, o, ln, dl, st, hb, kn, vn, kt, pb, dsb, g, g0, r0, sb, rb, dqt, dqi, dq, dk, dv,
    in_sem, out_sem, ps_sem, pr_sem, hs_sem, hr_sem, gs_sem, gr_sem, qs_sem, qr_sem, re_sem,
):
    part = q.shape[2]
    rows = 2 * part
    heads = dqt.shape[1]
    dim = dqt.shape[3]
    half = dim // 2
    n_ctx = lax.axis_size("ctx")
    scale = dim ** (-0.5)
    me = lax.axis_index("ctx")
    head = lax.axis_index("head")
    core = lax.rem(head, 2)
    ring = lax.rem(me, SPAN)
    base = head - core
    pair = base + 1 - core

    pieces = []
    for i in range(2):
        at = pl.ds(i * part, part)
        pieces += [
            (k_hbm.at[:, at], kv.at[i, 0:half]),
            (v_hbm.at[:, at], kv.at[i, half:dim]),
            (q_hbm.at[at], q.at[0, i]),
            (do_hbm.at[at], do.at[0, i]),
            (o_hbm.at[at], o.at[i]),
            (ln_hbm.at[:, at], ln.at[0, i]),
        ]
    loads = [pltpu.make_async_copy(s, d, in_sem.at[n]) for n, (s, d) in enumerate(pieces)]
    for c in loads:
        c.start()

    barrier = pltpu.get_barrier_semaphore()
    pl.semaphore_signal(barrier, inc=1, device_id=(me, pair), device_id_type=MESH)
    expected = jnp.int32(1)
    for d in range(1, SPAN + 1):

        @pl.when(me >= d)
        def _():
            for c in range(2):
                pl.semaphore_signal(
                    barrier, inc=1, device_id=(me - d, base + c), device_id_type=MESH
                )

        @pl.when(me + d < n_ctx)
        def _():
            for c in range(2):
                pl.semaphore_signal(
                    barrier, inc=1, device_id=(me + d, base + c), device_id_type=MESH
                )

        expected = expected + jnp.where(me >= d, 2, 0) + jnp.where(me + d < n_ctx, 2, 0)

    dqt[...] = jnp.zeros_like(dqt)
    g[0] = jnp.zeros(g.shape[1:], g.dtype)
    g[SPAN] = jnp.zeros(g.shape[1:], g.dtype)

    places = [
        me * rows + i * part + lax.broadcasted_iota(jnp.int32, (1, part), 1) for i in range(2)
    ]

    def one_doc(j, carry):
        end, a, b = carry
        end = end + doc_ref[j]
        return end, jnp.where(places[0] >= end, end, a), jnp.where(places[1] >= end, end, b)

    none = jnp.zeros((1, part), jnp.int32)
    _, st[0], st[1] = lax.fori_loop(0, doc_ref.shape[0], one_doc, (jnp.int32(0), none, none))

    for c in loads:
        c.wait()
    hb[0, core] = kv[core]

    for i in range(2):
        for h in range(heads):
            cols = slice(h * dim, (h + 1) * dim)
            prod = do[0, i, :, cols].astype(jnp.float32) * o[i, :, cols].astype(jnp.float32)
            dl[0, i, h : h + 1, :] = jnp.sum(prod.T, axis=0, keepdims=True)

    pl.semaphore_wait(barrier, expected)

    def remote(src, dst, send, recv, ctx, dev):
        return pltpu.make_async_remote_copy(
            src, dst, send, recv, device_id=(ctx, dev), device_id_type=MESH
        )

    swaps = [
        remote(s, d, ps_sem.at[n], pr_sem.at[n], me, pair)
        for n, (s, d) in enumerate(
            (
                (kv.at[1 - core], hb.at[0, core]),
                (q.at[0], q.at[1]),
                (do.at[0], do.at[1]),
                (ln.at[0], ln.at[1]),
                (dl.at[0], dl.at[1]),
                (g0.at[1 - core], r0),
            )
        )
    ]

    def ahead(d, c):
        return remote(
            kv.at[c], hb.at[d, core], hs_sem.at[d - 1, c], hr_sem.at[d - 1, core],
            me + d, base + c,
        )

    def arrived(d, s):
        return remote(
            kv.at[0], hb.at[d, s], hs_sem.at[d - 1, 0], hr_sem.at[d - 1, s], me, pair
        )

    def sends(d):
        near = me + d < n_ctx
        return near & (ring + d < SPAN) if d in RELAY else near

    def onward(d, s):
        return remote(
            hb.at[SPAN, s], hb.at[d, s], re_sem.at[d - RELAY[0], s], hr_sem.at[d - 1, s],
            me + d - SPAN, head,
        )

    def back(d, c):
        return remote(
            sb.at[d - 1, c], rb.at[d - 1, core], gs_sem.at[d - 1, c], gr_sem.at[d - 1, core],
            me - d, base + c,
        )

    def returned(d, s):
        return remote(
            sb.at[d - 1, 0], rb.at[d - 1, s], gs_sem.at[d - 1, 0], gr_sem.at[d - 1, s], me, pair
        )

    def hand(h):
        return remote(dqt.at[1, h], dqi.at[h], qs_sem.at[h], qr_sem.at[h], me, pair)

    swaps[0].start()
    for d in GATHER:

        @pl.when(sends(d))
        def _():
            for c in range(2):
                ahead(d, c).start()

    for c in swaps[1:5]:
        c.start()

    def await_block(d):
        @pl.when(me >= d)
        def _():
            for s in range(2):
                arrived(d, s).wait_recv()

        @pl.when(me < d)
        def _():
            hb[d] = jnp.zeros(hb.shape[1:], hb.dtype)

    def take(d):
        kt[...] = jnp.concatenate([hb[d, 0, :half], hb[d, 1, :half]], axis=0)
        kn[...] = kt[...].T
        vn[...] = jnp.concatenate([hb[d, 0, half:], hb[d, 1, half:]], axis=0).T

    krow = lax.broadcasted_iota(jnp.int32, (part, part), 0)
    qcol = lax.broadcasted_iota(jnp.int32, (part, part), 1)

    def attend(d, slot, halves, causal, fresh, between=None):
        first = (me - d) * rows + core * part
        for h in range(heads):
            cols = slice(h * dim, (h + 1) * dim)
            for n, i in enumerate(halves):
                s = mm(kn[...], q[slot, i, :, cols], NT)
                dp = mm(vn[...], do[slot, i, :, cols], NT)
                allowed = krow >= st[i] - first
                if causal:
                    allowed = allowed & (krow <= qcol)
                p = jnp.where(
                    allowed,
                    jnp.exp2(s * (scale * LOG2E) - ln[slot, i, h : h + 1, :] * LOG2E),
                    0.0,
                )
                pb[h, n] = p.astype(jnp.bfloat16)
                dsb[h, n] = (p * (dp - dl[slot, i, h : h + 1, :])).astype(jnp.bfloat16)
        if between is not None:
            between()
        gk, gv = (0.0, 0.0) if fresh else (g[d, 0], g[d, 1])
        for h in range(heads):
            cols = slice(h * dim, (h + 1) * dim)
            for n, i in enumerate(halves):
                gk = gk + mm(dsb[h, n], q[slot, i, :, cols], NN)
                gv = gv + mm(pb[h, n], do[slot, i, :, cols], NN)
                dqt[slot, h, i] += mm(kt[...], dsb[h, n], NN)
        g[d, 0], g[d, 1] = gk, gv

    def lay(dst, d):
        gk, gv = g[d, 0].T, g[d, 1].T
        for c in range(2):
            dst[c, 0:half] = gk[c * half : (c + 1) * half].astype(dst.dtype)
            dst[c, half:dim] = gv[c * half : (c + 1) * half].astype(dst.dtype)

    def give(d):
        @pl.when(me >= d)
        def _():
            for c in range(2):
                back(d, c).start()

    swaps[0].wait_recv()
    take(0)
    attend(0, 0, (core,), True, False)
    for c in swaps[1:5]:
        c.wait_recv()
    attend(0, 1, (core,), True, False)

    await_block(SPAN)
    for d in RELAY:

        @pl.when((ring + d >= SPAN) & (me >= SPAN))
        def _():
            for s in range(2):
                onward(d, s).start()

    side = SPAN * core
    take(side)
    for slot in range(2):
        attend(side, slot, (1 - core,), False, False)
    lay(g0, 0)

    pending = None
    for d in BLOCKS:
        await_block(d)
        take(d)
        if pending is None:
            swaps[5].start()
        else:
            give(pending)
        for slot in range(2):
            attend(d, slot, (0, 1), False, slot == 0)
        lay(sb.at[d - 1], d)
        pending = d

    take(SPAN)
    give(pending)
    attend(SPAN, 1, (core,), False, False)

    def hand_over():
        for h in range(heads):
            hand(h).start()

    attend(SPAN, 0, (core,), False, False, hand_over)
    lay(sb.at[SPAN - 1], SPAN)

    stores = []
    for i in range(2):
        at = pl.ds(i * part, part)
        stores += [(dq.at[i], dq_hbm.at[at]), (dk.at[i], dk_hbm.at[:, at]), (dv.at[i], dv_hbm.at[:, at])]
    stores = [pltpu.make_async_copy(s, d, out_sem.at[n]) for n, (s, d) in enumerate(stores)]

    for h in range(heads):
        hand(h).wait_recv()
        if h == 0:
            give(SPAN)
        for i in range(2):
            dq[i, :, h * dim : (h + 1) * dim] = (
                (dqt[0, h, i] + dqi[h, i]).T * scale
            ).astype(jnp.bfloat16)
    stores[0].start()
    stores[3].start()

    swaps[5].wait_recv()
    sums = [g0[core], r0[...]]
    for d in RETURN:

        @pl.when(me + d < n_ctx)
        def _():
            for s in range(2):
                returned(d, s).wait_recv()

        @pl.when(me + d >= n_ctx)
        def _():
            rb[d - 1] = jnp.zeros(rb.shape[1:], rb.dtype)

        sums[0] = sums[0] + rb[d - 1, core].astype(jnp.float32)
        sums[1] = sums[1] + rb[d - 1, 1 - core].astype(jnp.float32)
    for i, total in ((core, sums[0]), (1 - core, sums[1])):
        dk[i] = (total[:half] * scale).astype(jnp.bfloat16)
        dv[i] = total[half:].astype(jnp.bfloat16)
    for n in (1, 2, 4, 5):
        stores[n].start()

    for c in swaps:
        c.wait_send()
    for h in range(heads):
        hand(h).wait_send()
    for d in range(1, SPAN + 1):

        @pl.when(sends(d))
        def _():
            for c in range(2):
                ahead(d, c).wait_send()

        @pl.when(me >= d)
        def _():
            for c in range(2):
                back(d, c).wait_send()

    for d in RELAY:

        @pl.when((ring + d >= SPAN) & (me >= SPAN))
        def _():
            for s in range(2):
                onward(d, s).wait_send()

    for c in stores:
        c.wait()


def finish(dq, dk, dv, dq_out, dk_out, dv_out, q_buf, k_buf, v_buf, in_sem, out_sem):
    size = q_buf.shape[0] // 4
    hops = [(dk, k_buf, dk_out), (dv, v_buf, dv_out)]
    for n in range(4):
        at = pl.ds(n * size, size)
        hops.append((dq.at[at], q_buf.at[at], dq_out.at[at]))
    loads = [pltpu.make_async_copy(a, b, in_sem.at[n]) for n, (a, b, _) in enumerate(hops)]
    stores = [pltpu.make_async_copy(b, c, out_sem.at[n]) for n, (_, b, c) in enumerate(hops)]
    for c in loads:
        c.start()
    for a, b in zip(loads, stores):
        a.wait()
        b.start()
    for c in stores:
        c.wait()


def local(queries, key_states, value_states, attn_out, grad_out, log_norm, doc_lengths):
    rows, half = key_states.shape
    dim = 2 * half
    part = rows // 2
    heads = queries.shape[1] // dim
    wide = heads * dim
    bf, f32 = jnp.bfloat16, jnp.float32
    blocks = SPAN + 1
    anywhere = pl.BlockSpec(memory_space=pl.ANY)
    vmem, dma = pltpu.VMEM, pltpu.SemaphoreType.DMA
    grad_q, grad_k, grad_v = pl.pallas_call(
        kernel,
        out_shape=(
            jax.ShapeDtypeStruct((rows, wide), bf),
            jax.ShapeDtypeStruct((half, rows), bf),
            jax.ShapeDtypeStruct((half, rows), bf),
        ),
        in_specs=[pl.BlockSpec(memory_space=pltpu.SMEM)] + [anywhere] * 6,
        out_specs=(anywhere,) * 3,
        scratch_shapes=[
            vmem((2, dim, part), bf),
            vmem((2, 2, part, wide), bf),
            vmem((2, 2, part, wide), bf),
            vmem((2, part, wide), bf),
            vmem((2, 2, heads, part), f32),
            vmem((2, 2, heads, part), f32),
            vmem((2, 1, part), jnp.int32),
            vmem((blocks, 2, dim, part), bf),
            vmem((part, dim), bf),
            vmem((part, dim), bf),
            vmem((dim, part), bf),
            vmem((heads, 2, part, part), bf),
            vmem((heads, 2, part, part), bf),
            vmem((blocks, 2, part, dim), f32),
            vmem((2, dim, part), f32),
            vmem((dim, part), f32),
            vmem((SPAN, 2, dim, part), bf),
            vmem((SPAN, 2, dim, part), bf),
            vmem((2, heads, 2, dim, part), f32),
            vmem((heads, 2, dim, part), f32),
            vmem((2, part, wide), bf),
            vmem((2, half, part), bf),
            vmem((2, half, part), bf),
            dma((12,)), dma((6,)), dma((6,)), dma((6,)),
            dma((SPAN, 2)), dma((SPAN, 2)), dma((SPAN, 2)), dma((SPAN, 2)),
            dma((heads,)), dma((heads,)), dma((2, 2)),
        ],
        compiler_params=pltpu.CompilerParams(
            collective_id=0, has_side_effects=True, vmem_limit_bytes=60 * 2**20
        ),
    )(doc_lengths, queries, key_states.T, value_states.T, attn_out, grad_out, log_norm)
    grad_q, grad_k, grad_v = pl.pallas_call(
        finish,
        out_shape=(
            jax.ShapeDtypeStruct((rows, wide), bf),
            jax.ShapeDtypeStruct((half, rows), bf),
            jax.ShapeDtypeStruct((half, rows), bf),
        ),
        in_specs=[anywhere] * 3,
        out_specs=(anywhere,) * 3,
        scratch_shapes=[
            vmem((rows, wide), bf), vmem((half, rows), bf), vmem((half, rows), bf),
            dma((6,)), dma((6,)),
        ],
        compiler_params=pltpu.CompilerParams(vmem_limit_bytes=60 * 2**20),
    )(grad_q, grad_k, grad_v)
    return grad_q, grad_k.T, grad_v.T


def solution(mesh):
    in_specs = (
        P("ctx", "head"), P("ctx", "head"), P("ctx", "head"), P("ctx", "head"),
        P("ctx", "head"), P("head", "ctx"), P(),
    )
    out_specs = (P("ctx", "head"), P("ctx", "head"), P("ctx", "head"))
    return jax.shard_map(local, mesh=mesh, in_specs=in_specs, out_specs=out_specs, check_vma=False)
```

```python
import jax
import jax.numpy as jnp
from jax import lax
from jax.experimental import pallas as pl
from jax.experimental.pallas import tpu as pltpu
from jax.sharding import PartitionSpec as P

MESH = pl.DeviceIdType.MESH
LOG2E = 1.4426950408889634
NT = (((1,), (1,)), ((), ()))
NN = (((1,), (0,)), ((), ()))
SPAN = 4
GATHER = (4, 1, 3, 2)
BLOCKS = (1, 3, 2)
RETURN = (1, 3, 2, 4)
RELAY = (2, 3)


def mm(a, b, dims):
    return lax.dot_general(a, b, dims, preferred_element_type=jnp.float32)


def kernel(
    doc_ref, q_hbm, k_hbm, v_hbm, o_hbm, do_hbm, ln_hbm,
    dq_hbm, dk_hbm, dv_hbm,
    kv, q, do, o, ln, dl, st, hb, kn, vn, kt, pb, dsb, g, g0, r0, sb, rb, dqt, dqi, dq, dk, dv,
    in_sem, out_sem, ps_sem, pr_sem, hs_sem, hr_sem, gs_sem, gr_sem, qs_sem, qr_sem, re_sem,
):
    part = q.shape[2]
    rows = 2 * part
    heads = dqt.shape[1]
    dim = dqt.shape[3]
    half = dim // 2
    n_ctx = lax.axis_size("ctx")
    scale = dim ** (-0.5)
    me = lax.axis_index("ctx")
    head = lax.axis_index("head")
    core = lax.rem(head, 2)
    ring = lax.rem(me, SPAN)
    base = head - core
    pair = base + 1 - core

    pieces = []
    for i in range(2):
        at = pl.ds(i * part, part)
        pieces += [
            (k_hbm.at[:, at], kv.at[i, 0:half]),
            (v_hbm.at[:, at], kv.at[i, half:dim]),
            (q_hbm.at[at], q.at[0, i]),
            (do_hbm.at[at], do.at[0, i]),
            (o_hbm.at[at], o.at[i]),
            (ln_hbm.at[:, at], ln.at[0, i]),
        ]
    loads = [pltpu.make_async_copy(s, d, in_sem.at[n]) for n, (s, d) in enumerate(pieces)]
    for c in loads:
        c.start()

    barrier = pltpu.get_barrier_semaphore()
    pl.semaphore_signal(barrier, inc=1, device_id=(me, pair), device_id_type=MESH)
    expected = jnp.int32(1)
    for d in range(1, SPAN + 1):

        @pl.when(me >= d)
        def _():
            for c in range(2):
                pl.semaphore_signal(
                    barrier, inc=1, device_id=(me - d, base + c), device_id_type=MESH
                )

        @pl.when(me + d < n_ctx)
        def _():
            for c in range(2):
                pl.semaphore_signal(
                    barrier, inc=1, device_id=(me + d, base + c), device_id_type=MESH
                )

        expected = expected + jnp.where(me >= d, 2, 0) + jnp.where(me + d < n_ctx, 2, 0)

    dqt[...] = jnp.zeros_like(dqt)
    g[0] = jnp.zeros(g.shape[1:], g.dtype)
    g[SPAN] = jnp.zeros(g.shape[1:], g.dtype)

    places = [
        me * rows + i * part + lax.broadcasted_iota(jnp.int32, (1, part), 1) for i in range(2)
    ]

    def one_doc(j, carry):
        end, a, b = carry
        end = end + doc_ref[j]
        return end, jnp.where(places[0] >= end, end, a), jnp.where(places[1] >= end, end, b)

    none = jnp.zeros((1, part), jnp.int32)
    _, st[0], st[1] = lax.fori_loop(0, doc_ref.shape[0], one_doc, (jnp.int32(0), none, none))

    for c in loads:
        c.wait()
    hb[0, core] = kv[core]

    for i in range(2):
        for h in range(heads):
            cols = slice(h * dim, (h + 1) * dim)
            prod = do[0, i, :, cols].astype(jnp.float32) * o[i, :, cols].astype(jnp.float32)
            dl[0, i, h : h + 1, :] = jnp.sum(prod.T, axis=0, keepdims=True)

    pl.semaphore_wait(barrier, expected)

    def remote(src, dst, send, recv, ctx, dev):
        return pltpu.make_async_remote_copy(
            src, dst, send, recv, device_id=(ctx, dev), device_id_type=MESH
        )

    swaps = [
        remote(s, d, ps_sem.at[n], pr_sem.at[n], me, pair)
        for n, (s, d) in enumerate(
            (
                (kv.at[1 - core], hb.at[0, core]),
                (q.at[0], q.at[1]),
                (do.at[0], do.at[1]),
                (ln.at[0], ln.at[1]),
                (dl.at[0], dl.at[1]),
                (g0.at[1 - core], r0),
            )
        )
    ]

    def ahead(d, c):
        return remote(
            kv.at[c], hb.at[d, core], hs_sem.at[d - 1, c], hr_sem.at[d - 1, core],
            me + d, base + c,
        )

    def arrived(d, s):
        return remote(
            kv.at[0], hb.at[d, s], hs_sem.at[d - 1, 0], hr_sem.at[d - 1, s], me, pair
        )

    def sends(d):
        near = me + d < n_ctx
        return near & (ring + d < SPAN) if d in RELAY else near

    def onward(d, s):
        return remote(
            hb.at[SPAN, s], hb.at[d, s], re_sem.at[d - RELAY[0], s], hr_sem.at[d - 1, s],
            me + d - SPAN, head,
        )

    def back(d, c):
        return remote(
            sb.at[d - 1, c], rb.at[d - 1, core], gs_sem.at[d - 1, c], gr_sem.at[d - 1, core],
            me - d, base + c,
        )

    def returned(d, s):
        return remote(
            sb.at[d - 1, 0], rb.at[d - 1, s], gs_sem.at[d - 1, 0], gr_sem.at[d - 1, s], me, pair
        )

    def hand(h):
        return remote(dqt.at[1, h], dqi.at[h], qs_sem.at[h], qr_sem.at[h], me, pair)

    swaps[0].start()
    for d in GATHER:

        @pl.when(sends(d))
        def _():
            for c in range(2):
                ahead(d, c).start()

    for c in swaps[1:5]:
        c.start()

    def await_block(d):
        @pl.when(me >= d)
        def _():
            for s in range(2):
                arrived(d, s).wait_recv()

        @pl.when(me < d)
        def _():
            hb[d] = jnp.zeros(hb.shape[1:], hb.dtype)

    def take(d):
        kt[...] = jnp.concatenate([hb[d, 0, :half], hb[d, 1, :half]], axis=0)
        kn[...] = kt[...].T
        vn[...] = jnp.concatenate([hb[d, 0, half:], hb[d, 1, half:]], axis=0).T

    krow = lax.broadcasted_iota(jnp.int32, (part, part), 0)
    qcol = lax.broadcasted_iota(jnp.int32, (part, part), 1)

    def attend(d, slot, halves, causal, fresh, between=None):
        first = (me - d) * rows + core * part
        for h in range(heads):
            cols = slice(h * dim, (h + 1) * dim)
            for n, i in enumerate(halves):
                s = mm(kn[...], q[slot, i, :, cols], NT)
                dp = mm(vn[...], do[slot, i, :, cols], NT)
                allowed = krow >= st[i] - first
                if causal:
                    allowed = allowed & (krow <= qcol)
                p = jnp.where(
                    allowed,
                    jnp.exp2(s * (scale * LOG2E) - ln[slot, i, h : h + 1, :] * LOG2E),
                    0.0,
                )
                pb[h, n] = p.astype(jnp.bfloat16)
                dsb[h, n] = (p * (dp - dl[slot, i, h : h + 1, :])).astype(jnp.bfloat16)
        if between is not None:
            between()
        gk, gv = (0.0, 0.0) if fresh else (g[d, 0], g[d, 1])
        for h in range(heads):
            cols = slice(h * dim, (h + 1) * dim)
            for n, i in enumerate(halves):
                gk = gk + mm(dsb[h, n], q[slot, i, :, cols], NN)
                gv = gv + mm(pb[h, n], do[slot, i, :, cols], NN)
                dqt[slot, h, i] += mm(kt[...], dsb[h, n], NN)
        g[d, 0], g[d, 1] = gk, gv

    def lay(dst, d):
        gk, gv = g[d, 0].T, g[d, 1].T
        for c in range(2):
            dst[c, 0:half] = gk[c * half : (c + 1) * half].astype(dst.dtype)
            dst[c, half:dim] = gv[c * half : (c + 1) * half].astype(dst.dtype)

    def give(d):
        @pl.when(me >= d)
        def _():
            for c in range(2):
                back(d, c).start()

    swaps[0].wait_recv()
    take(0)
    attend(0, 0, (core,), True, False)
    for c in swaps[1:5]:
        c.wait_recv()
    attend(0, 1, (core,), True, False)

    await_block(SPAN)
    for d in RELAY:

        @pl.when((ring + d >= SPAN) & (me >= SPAN))
        def _():
            for s in range(2):
                onward(d, s).start()

    side = SPAN * core
    take(side)
    for slot in range(2):
        attend(side, slot, (1 - core,), False, False)
    lay(g0, 0)

    pending = None
    for d in BLOCKS:
        await_block(d)
        take(d)
        if pending is None:
            swaps[5].start()
        else:
            give(pending)
        for slot in range(2):
            attend(d, slot, (0, 1), False, slot == 0)
        lay(sb.at[d - 1], d)
        pending = d

    take(SPAN)
    give(pending)
    attend(SPAN, 1, (core,), False, False)

    def hand_over():
        for h in range(heads):
            hand(h).start()

    attend(SPAN, 0, (core,), False, False, hand_over)
    lay(sb.at[SPAN - 1], SPAN)

    swaps[5].wait_recv()
    give(SPAN)

    stores = []
    for i in range(2):
        at = pl.ds(i * part, part)
        stores += [(dq.at[i], dq_hbm.at[at]), (dk.at[i], dk_hbm.at[:, at]), (dv.at[i], dv_hbm.at[:, at])]
    stores = [pltpu.make_async_copy(s, d, out_sem.at[n]) for n, (s, d) in enumerate(stores)]

    for h in range(heads):
        hand(h).wait_recv()
        for i in range(2):
            dq[i, :, h * dim : (h + 1) * dim] = (
                (dqt[0, h, i] + dqi[h, i]).T * scale
            ).astype(jnp.bfloat16)
    stores[0].start()
    stores[3].start()

    sums = [g0[core], r0[...]]
    for d in RETURN:

        @pl.when(me + d < n_ctx)
        def _():
            for s in range(2):
                returned(d, s).wait_recv()

        @pl.when(me + d >= n_ctx)
        def _():
            rb[d - 1] = jnp.zeros(rb.shape[1:], rb.dtype)

        sums[0] = sums[0] + rb[d - 1, core].astype(jnp.float32)
        sums[1] = sums[1] + rb[d - 1, 1 - core].astype(jnp.float32)
    for i, total in ((core, sums[0]), (1 - core, sums[1])):
        dk[i] = (total[:half] * scale).astype(jnp.bfloat16)
        dv[i] = total[half:].astype(jnp.bfloat16)
    for n in (1, 2, 4, 5):
        stores[n].start()

    for c in swaps:
        c.wait_send()
    for h in range(heads):
        hand(h).wait_send()
    for d in range(1, SPAN + 1):

        @pl.when(sends(d))
        def _():
            for c in range(2):
                ahead(d, c).wait_send()

        @pl.when(me >= d)
        def _():
            for c in range(2):
                back(d, c).wait_send()

    for d in RELAY:

        @pl.when((ring + d >= SPAN) & (me >= SPAN))
        def _():
            for s in range(2):
                onward(d, s).wait_send()

    for c in stores:
        c.wait()


def finish(dq, dk, dv, dq_out, dk_out, dv_out, q_buf, k_buf, v_buf, in_sem, out_sem):
    size = q_buf.shape[0] // 4
    hops = [(dk, k_buf, dk_out), (dv, v_buf, dv_out)]
    for n in range(4):
        at = pl.ds(n * size, size)
        hops.append((dq.at[at], q_buf.at[at], dq_out.at[at]))
    loads = [pltpu.make_async_copy(a, b, in_sem.at[n]) for n, (a, b, _) in enumerate(hops)]
    stores = [pltpu.make_async_copy(b, c, out_sem.at[n]) for n, (_, b, c) in enumerate(hops)]
    for c in loads:
        c.start()
    for a, b in zip(loads, stores):
        a.wait()
        b.start()
    for c in stores:
        c.wait()


def local(queries, key_states, value_states, attn_out, grad_out, log_norm, doc_lengths):
    rows, half = key_states.shape
    dim = 2 * half
    part = rows // 2
    heads = queries.shape[1] // dim
    wide = heads * dim
    bf, f32 = jnp.bfloat16, jnp.float32
    blocks = SPAN + 1
    anywhere = pl.BlockSpec(memory_space=pl.ANY)
    vmem, dma = pltpu.VMEM, pltpu.SemaphoreType.DMA
    grad_q, grad_k, grad_v = pl.pallas_call(
        kernel,
        out_shape=(
            jax.ShapeDtypeStruct((rows, wide), bf),
            jax.ShapeDtypeStruct((half, rows), bf),
            jax.ShapeDtypeStruct((half, rows), bf),
        ),
        in_specs=[pl.BlockSpec(memory_space=pltpu.SMEM)] + [anywhere] * 6,
        out_specs=(anywhere,) * 3,
        scratch_shapes=[
            vmem((2, dim, part), bf),
            vmem((2, 2, part, wide), bf),
            vmem((2, 2, part, wide), bf),
            vmem((2, part, wide), bf),
            vmem((2, 2, heads, part), f32),
            vmem((2, 2, heads, part), f32),
            vmem((2, 1, part), jnp.int32),
            vmem((blocks, 2, dim, part), bf),
            vmem((part, dim), bf),
            vmem((part, dim), bf),
            vmem((dim, part), bf),
            vmem((heads, 2, part, part), bf),
            vmem((heads, 2, part, part), bf),
            vmem((blocks, 2, part, dim), f32),
            vmem((2, dim, part), f32),
            vmem((dim, part), f32),
            vmem((SPAN, 2, dim, part), bf),
            vmem((SPAN, 2, dim, part), bf),
            vmem((2, heads, 2, dim, part), f32),
            vmem((heads, 2, dim, part), f32),
            vmem((2, part, wide), bf),
            vmem((2, half, part), bf),
            vmem((2, half, part), bf),
            dma((12,)), dma((6,)), dma((6,)), dma((6,)),
            dma((SPAN, 2)), dma((SPAN, 2)), dma((SPAN, 2)), dma((SPAN, 2)),
            dma((heads,)), dma((heads,)), dma((2, 2)),
        ],
        compiler_params=pltpu.CompilerParams(
            collective_id=0, has_side_effects=True, vmem_limit_bytes=60 * 2**20
        ),
    )(doc_lengths, queries, key_states.T, value_states.T, attn_out, grad_out, log_norm)
    grad_q, grad_k, grad_v = pl.pallas_call(
        finish,
        out_shape=(
            jax.ShapeDtypeStruct((rows, wide), bf),
            jax.ShapeDtypeStruct((half, rows), bf),
            jax.ShapeDtypeStruct((half, rows), bf),
        ),
        in_specs=[anywhere] * 3,
        out_specs=(anywhere,) * 3,
        scratch_shapes=[
            vmem((rows, wide), bf), vmem((half, rows), bf), vmem((half, rows), bf),
            dma((6,)), dma((6,)),
        ],
        compiler_params=pltpu.CompilerParams(vmem_limit_bytes=60 * 2**20),
    )(grad_q, grad_k, grad_v)
    return grad_q, grad_k.T, grad_v.T


def solution(mesh):
    in_specs = (
        P("ctx", "head"), P("ctx", "head"), P("ctx", "head"), P("ctx", "head"),
        P("ctx", "head"), P("head", "ctx"), P(),
    )
    out_specs = (P("ctx", "head"), P("ctx", "head"), P("ctx", "head"))
    return jax.shard_map(local, mesh=mesh, in_specs=in_specs, out_specs=out_specs, check_vma=False)
```

```python
import jax
import jax.numpy as jnp
from jax import lax
from jax.experimental import pallas as pl
from jax.experimental.pallas import tpu as pltpu
from jax.sharding import PartitionSpec as P

MESH = pl.DeviceIdType.MESH
LOG2E = 1.4426950408889634
NT = (((1,), (1,)), ((), ()))
NN = (((1,), (0,)), ((), ()))
SPAN = 4
GATHER = (4, 1, 3, 2)
BLOCKS = (1, 3, 2)
RETURN = (4, 1, 3, 2)
RELAY = (2, 3)


def mm(a, b, dims):
    return lax.dot_general(a, b, dims, preferred_element_type=jnp.float32)


def kernel(
    doc_ref, q_hbm, k_hbm, v_hbm, o_hbm, do_hbm, ln_hbm,
    dq_hbm, dk_hbm, dv_hbm,
    kv, q, do, o, ln, dl, st, hb, kn, vn, kt, pb, dsb, g, g0, r0, sb, rb, dqt, dqi, dq, dk, dv,
    in_sem, out_sem, ps_sem, pr_sem, hs_sem, hr_sem, gs_sem, gr_sem, qs_sem, qr_sem, re_sem,
):
    part = q.shape[2]
    rows = 2 * part
    heads = dqt.shape[1]
    dim = dqt.shape[3]
    half = dim // 2
    n_ctx = lax.axis_size("ctx")
    scale = dim ** (-0.5)
    me = lax.axis_index("ctx")
    head = lax.axis_index("head")
    core = lax.rem(head, 2)
    ring = lax.rem(me, SPAN)
    base = head - core
    pair = base + 1 - core

    pieces = []
    for i in range(2):
        at = pl.ds(i * part, part)
        pieces += [
            (k_hbm.at[:, at], kv.at[i, 0:half]),
            (v_hbm.at[:, at], kv.at[i, half:dim]),
            (q_hbm.at[at], q.at[0, i]),
            (do_hbm.at[at], do.at[0, i]),
            (o_hbm.at[at], o.at[i]),
            (ln_hbm.at[:, at], ln.at[0, i]),
        ]
    loads = [pltpu.make_async_copy(s, d, in_sem.at[n]) for n, (s, d) in enumerate(pieces)]
    for c in loads:
        c.start()

    barrier = pltpu.get_barrier_semaphore()
    pl.semaphore_signal(barrier, inc=1, device_id=(me, pair), device_id_type=MESH)
    expected = jnp.int32(1)
    for d in range(1, SPAN + 1):

        @pl.when(me >= d)
        def _():
            for c in range(2):
                pl.semaphore_signal(
                    barrier, inc=1, device_id=(me - d, base + c), device_id_type=MESH
                )

        @pl.when(me + d < n_ctx)
        def _():
            for c in range(2):
                pl.semaphore_signal(
                    barrier, inc=1, device_id=(me + d, base + c), device_id_type=MESH
                )

        expected = expected + jnp.where(me >= d, 2, 0) + jnp.where(me + d < n_ctx, 2, 0)

    dqt[...] = jnp.zeros_like(dqt)
    g[0] = jnp.zeros(g.shape[1:], g.dtype)
    g[SPAN] = jnp.zeros(g.shape[1:], g.dtype)

    places = [
        me * rows + i * part + lax.broadcasted_iota(jnp.int32, (1, part), 1) for i in range(2)
    ]

    def one_doc(j, carry):
        end, a, b = carry
        end = end + doc_ref[j]
        return end, jnp.where(places[0] >= end, end, a), jnp.where(places[1] >= end, end, b)

    none = jnp.zeros((1, part), jnp.int32)
    _, st[0], st[1] = lax.fori_loop(0, doc_ref.shape[0], one_doc, (jnp.int32(0), none, none))

    for c in loads:
        c.wait()
    hb[0, core] = kv[core]

    for i in range(2):
        for h in range(heads):
            cols = slice(h * dim, (h + 1) * dim)
            prod = do[0, i, :, cols].astype(jnp.float32) * o[i, :, cols].astype(jnp.float32)
            dl[0, i, h : h + 1, :] = jnp.sum(prod.T, axis=0, keepdims=True)

    pl.semaphore_wait(barrier, expected)

    def remote(src, dst, send, recv, ctx, dev):
        return pltpu.make_async_remote_copy(
            src, dst, send, recv, device_id=(ctx, dev), device_id_type=MESH
        )

    swaps = [
        remote(s, d, ps_sem.at[n], pr_sem.at[n], me, pair)
        for n, (s, d) in enumerate(
            (
                (kv.at[1 - core], hb.at[0, core]),
                (q.at[0], q.at[1]),
                (do.at[0], do.at[1]),
                (ln.at[0], ln.at[1]),
                (dl.at[0], dl.at[1]),
                (g0.at[1 - core], r0),
            )
        )
    ]

    def ahead(d, c):
        return remote(
            kv.at[c], hb.at[d, core], hs_sem.at[d - 1, c], hr_sem.at[d - 1, core],
            me + d, base + c,
        )

    def arrived(d, s):
        return remote(
            kv.at[0], hb.at[d, s], hs_sem.at[d - 1, 0], hr_sem.at[d - 1, s], me, pair
        )

    def sends(d):
        near = me + d < n_ctx
        return near & (ring + d < SPAN) if d in RELAY else near

    def onward(d, s):
        return remote(
            hb.at[SPAN, s], hb.at[d, s], re_sem.at[d - RELAY[0], s], hr_sem.at[d - 1, s],
            me + d - SPAN, head,
        )

    def back(d, c):
        return remote(
            sb.at[d - 1, c], rb.at[d - 1, core], gs_sem.at[d - 1, c], gr_sem.at[d - 1, core],
            me - d, base + c,
        )

    def returned(d, s):
        return remote(
            sb.at[d - 1, 0], rb.at[d - 1, s], gs_sem.at[d - 1, 0], gr_sem.at[d - 1, s], me, pair
        )

    def hand(h):
        return remote(dqt.at[1, h], dqi.at[h], qs_sem.at[h], qr_sem.at[h], me, pair)

    swaps[0].start()
    for d in GATHER:

        @pl.when(sends(d))
        def _():
            for c in range(2):
                ahead(d, c).start()

    for c in swaps[1:5]:
        c.start()

    def await_block(d):
        @pl.when(me >= d)
        def _():
            for s in range(2):
                arrived(d, s).wait_recv()

        @pl.when(me < d)
        def _():
            hb[d] = jnp.zeros(hb.shape[1:], hb.dtype)

    def take(d):
        kt[...] = jnp.concatenate([hb[d, 0, :half], hb[d, 1, :half]], axis=0)
        kn[...] = kt[...].T
        vn[...] = jnp.concatenate([hb[d, 0, half:], hb[d, 1, half:]], axis=0).T

    krow = lax.broadcasted_iota(jnp.int32, (part, part), 0)
    qcol = lax.broadcasted_iota(jnp.int32, (part, part), 1)

    def attend(d, slot, halves, causal, fresh, between=None):
        first = (me - d) * rows + core * part
        for h in range(heads):
            cols = slice(h * dim, (h + 1) * dim)
            for n, i in enumerate(halves):
                s = mm(kn[...], q[slot, i, :, cols], NT)
                dp = mm(vn[...], do[slot, i, :, cols], NT)
                allowed = krow >= st[i] - first
                if causal:
                    allowed = allowed & (krow <= qcol)
                p = jnp.where(
                    allowed,
                    jnp.exp2(s * (scale * LOG2E) - ln[slot, i, h : h + 1, :] * LOG2E),
                    0.0,
                )
                pb[h, n] = p.astype(jnp.bfloat16)
                dsb[h, n] = (p * (dp - dl[slot, i, h : h + 1, :])).astype(jnp.bfloat16)
        if between is not None:
            between()
        gk, gv = (0.0, 0.0) if fresh else (g[d, 0], g[d, 1])
        for h in range(heads):
            cols = slice(h * dim, (h + 1) * dim)
            for n, i in enumerate(halves):
                gk = gk + mm(dsb[h, n], q[slot, i, :, cols], NN)
                gv = gv + mm(pb[h, n], do[slot, i, :, cols], NN)
                dqt[slot, h, i] += mm(kt[...], dsb[h, n], NN)
        g[d, 0], g[d, 1] = gk, gv

    def lay(dst, d):
        gk, gv = g[d, 0].T, g[d, 1].T
        for c in range(2):
            dst[c, 0:half] = gk[c * half : (c + 1) * half].astype(dst.dtype)
            dst[c, half:dim] = gv[c * half : (c + 1) * half].astype(dst.dtype)

    def give(d):
        @pl.when(me >= d)
        def _():
            for c in range(2):
                back(d, c).start()

    swaps[0].wait_recv()
    take(0)
    attend(0, 0, (core,), True, False)
    for c in swaps[1:5]:
        c.wait_recv()
    attend(0, 1, (core,), True, False)

    await_block(SPAN)
    for d in RELAY:

        @pl.when((ring + d >= SPAN) & (me >= SPAN))
        def _():
            for s in range(2):
                onward(d, s).start()

    side = SPAN * core
    take(side)
    for slot in range(2):
        attend(side, slot, (1 - core,), False, False)
    lay(g0, 0)

    take(SPAN)
    swaps[5].start()
    for slot in range(2):
        attend(SPAN, slot, (core,), False, False)
    lay(sb.at[SPAN - 1], SPAN)

    def hand_over():
        for h in range(heads):
            hand(h).start()

    pending = SPAN
    for d in BLOCKS:
        await_block(d)
        take(d)
        give(pending)
        attend(d, 1, (0, 1), False, True)
        attend(d, 0, (0, 1), False, False, hand_over if d == BLOCKS[-1] else None)
        lay(sb.at[d - 1], d)
        pending = d
    swaps[5].wait_recv()
    give(pending)

    stores = []
    for i in range(2):
        at = pl.ds(i * part, part)
        stores += [(dq.at[i], dq_hbm.at[at]), (dk.at[i], dk_hbm.at[:, at]), (dv.at[i], dv_hbm.at[:, at])]
    stores = [pltpu.make_async_copy(s, d, out_sem.at[n]) for n, (s, d) in enumerate(stores)]

    for h in range(heads):
        hand(h).wait_recv()
        for i in range(2):
            dq[i, :, h * dim : (h + 1) * dim] = (
                (dqt[0, h, i] + dqi[h, i]).T * scale
            ).astype(jnp.bfloat16)
    stores[0].start()
    stores[3].start()

    sums = [g0[core], r0[...]]
    for d in RETURN:

        @pl.when(me + d < n_ctx)
        def _():
            for s in range(2):
                returned(d, s).wait_recv()

        @pl.when(me + d >= n_ctx)
        def _():
            rb[d - 1] = jnp.zeros(rb.shape[1:], rb.dtype)

        sums[0] = sums[0] + rb[d - 1, core].astype(jnp.float32)
        sums[1] = sums[1] + rb[d - 1, 1 - core].astype(jnp.float32)
    for i, total in ((core, sums[0]), (1 - core, sums[1])):
        dk[i] = (total[:half] * scale).astype(jnp.bfloat16)
        dv[i] = total[half:].astype(jnp.bfloat16)
    for n in (1, 2, 4, 5):
        stores[n].start()

    for c in swaps:
        c.wait_send()
    for h in range(heads):
        hand(h).wait_send()
    for d in range(1, SPAN + 1):

        @pl.when(sends(d))
        def _():
            for c in range(2):
                ahead(d, c).wait_send()

        @pl.when(me >= d)
        def _():
            for c in range(2):
                back(d, c).wait_send()

    for d in RELAY:

        @pl.when((ring + d >= SPAN) & (me >= SPAN))
        def _():
            for s in range(2):
                onward(d, s).wait_send()

    for c in stores:
        c.wait()


def finish(dq, dk, dv, dq_out, dk_out, dv_out, q_buf, k_buf, v_buf, in_sem, out_sem):
    size = q_buf.shape[0] // 4
    hops = [(dk, k_buf, dk_out), (dv, v_buf, dv_out)]
    for n in range(4):
        at = pl.ds(n * size, size)
        hops.append((dq.at[at], q_buf.at[at], dq_out.at[at]))
    loads = [pltpu.make_async_copy(a, b, in_sem.at[n]) for n, (a, b, _) in enumerate(hops)]
    stores = [pltpu.make_async_copy(b, c, out_sem.at[n]) for n, (_, b, c) in enumerate(hops)]
    for c in loads:
        c.start()
    for a, b in zip(loads, stores):
        a.wait()
        b.start()
    for c in stores:
        c.wait()


def local(queries, key_states, value_states, attn_out, grad_out, log_norm, doc_lengths):
    rows, half = key_states.shape
    dim = 2 * half
    part = rows // 2
    heads = queries.shape[1] // dim
    wide = heads * dim
    bf, f32 = jnp.bfloat16, jnp.float32
    blocks = SPAN + 1
    anywhere = pl.BlockSpec(memory_space=pl.ANY)
    vmem, dma = pltpu.VMEM, pltpu.SemaphoreType.DMA
    grad_q, grad_k, grad_v = pl.pallas_call(
        kernel,
        out_shape=(
            jax.ShapeDtypeStruct((rows, wide), bf),
            jax.ShapeDtypeStruct((half, rows), bf),
            jax.ShapeDtypeStruct((half, rows), bf),
        ),
        in_specs=[pl.BlockSpec(memory_space=pltpu.SMEM)] + [anywhere] * 6,
        out_specs=(anywhere,) * 3,
        scratch_shapes=[
            vmem((2, dim, part), bf),
            vmem((2, 2, part, wide), bf),
            vmem((2, 2, part, wide), bf),
            vmem((2, part, wide), bf),
            vmem((2, 2, heads, part), f32),
            vmem((2, 2, heads, part), f32),
            vmem((2, 1, part), jnp.int32),
            vmem((blocks, 2, dim, part), bf),
            vmem((part, dim), bf),
            vmem((part, dim), bf),
            vmem((dim, part), bf),
            vmem((heads, 2, part, part), bf),
            vmem((heads, 2, part, part), bf),
            vmem((blocks, 2, part, dim), f32),
            vmem((2, dim, part), f32),
            vmem((dim, part), f32),
            vmem((SPAN, 2, dim, part), bf),
            vmem((SPAN, 2, dim, part), bf),
            vmem((2, heads, 2, dim, part), f32),
            vmem((heads, 2, dim, part), f32),
            vmem((2, part, wide), bf),
            vmem((2, half, part), bf),
            vmem((2, half, part), bf),
            dma((12,)), dma((6,)), dma((6,)), dma((6,)),
            dma((SPAN, 2)), dma((SPAN, 2)), dma((SPAN, 2)), dma((SPAN, 2)),
            dma((heads,)), dma((heads,)), dma((2, 2)),
        ],
        compiler_params=pltpu.CompilerParams(
            collective_id=0, has_side_effects=True, vmem_limit_bytes=60 * 2**20
        ),
    )(doc_lengths, queries, key_states.T, value_states.T, attn_out, grad_out, log_norm)
    grad_q, grad_k, grad_v = pl.pallas_call(
        finish,
        out_shape=(
            jax.ShapeDtypeStruct((rows, wide), bf),
            jax.ShapeDtypeStruct((half, rows), bf),
            jax.ShapeDtypeStruct((half, rows), bf),
        ),
        in_specs=[anywhere] * 3,
        out_specs=(anywhere,) * 3,
        scratch_shapes=[
            vmem((rows, wide), bf), vmem((half, rows), bf), vmem((half, rows), bf),
            dma((6,)), dma((6,)),
        ],
        compiler_params=pltpu.CompilerParams(vmem_limit_bytes=60 * 2**20),
    )(grad_q, grad_k, grad_v)
    return grad_q, grad_k.T, grad_v.T


def solution(mesh):
    in_specs = (
        P("ctx", "head"), P("ctx", "head"), P("ctx", "head"), P("ctx", "head"),
        P("ctx", "head"), P("head", "ctx"), P(),
    )
    out_specs = (P("ctx", "head"), P("ctx", "head"), P("ctx", "head"))
    return jax.shard_map(local, mesh=mesh, in_specs=in_specs, out_specs=out_specs, check_vma=False)
```
